32 devices in a mesh: tm: 4 (over x, core), rows: 8 (over z, y).
Axes of the slice: x: 2, y: 2, z: 4, core: 2. Of those that a mesh axis runs over, the one named last changes fastest.
Arguments:
- latent: bfloat16 [8, 16, 160, 16], P('tm', 'rows'), may hold values from -6 to 6
- entry_kernel: bfloat16 [3, 3, 3, 16, 256], replicated, may hold values from -0.3125 to 0.3125
- middle_kernel: bfloat16 [3, 3, 3, 256, 256], replicated, may hold values from -0.078125 to 0.078125
- upper_kernel: bfloat16 [3, 3, 3, 256, 256], replicated, may hold values from -0.078125 to 0.078125
Outputs:
- decoded: bfloat16 [8, 32, 320, 256], P('tm', 'rows')
The draws below stay inside these ranges and needn't reach their ends.
All inputs are finite; a program needn't handle non-finite values.
Results may differ from the reference program's by a relative error of at most 0.0059.
Values may be sent and summed in bfloat16 or wider, within the bound.
No kernel may reach another device: no remote copies, remote signals or barrier semaphores. Data moves between devices by JAX's collectives and lax.ppermute only.
A program may use at most 64 MiB of HBM per device.

```python
import jax
import jax.numpy as jnp
from jax import lax

CIN = 16
CH = 256
W = 160
NT = 8
NH = 16


def level_of(stream_key, shape, shards, smallest, largest):
    loudness = 1.0
    for axis_at, parts in shards:
        steps = jax.random.uniform(jax.random.fold_in(jax.random.fold_in(stream_key, 6), axis_at), (parts,), jnp.float32, smallest / len(shards), largest / len(shards))
        loudness = loudness * jnp.repeat(jnp.exp(steps), shape[axis_at] // parts).reshape((-1,) + (1,) * (len(shape) - 1 - axis_at))
    return loudness


def centred(own_key, extent, width, bound, pieces=(), held_as=jnp.bfloat16):
    array = width * jax.random.normal(own_key, extent, jnp.float32)
    if pieces:
        array = array * level_of(own_key, extent, pieces, -0.22, 0.18)
    return jnp.clip(array, -bound, bound).astype(held_as)


def setup_inputs(seed: int = 0) -> dict:
    arg_keys = jax.random.split(jax.random.key(seed), 5)
    return {
        "latent": centred(arg_keys[0], (NT, NH, W, CIN), 1.0, 6.0, ((0, 4), (1, 8))),
        "entry_kernel": centred(arg_keys[1], (3, 3, 3, CIN, CH), (27 * CIN) ** -0.5, 0.3125),
        "middle_kernel": centred(arg_keys[2], (3, 3, 3, CH, CH), (27 * CH) ** -0.5, 0.078125),
        "upper_kernel": centred(arg_keys[3], (3, 3, 3, CH, CH), (27 * CH) ** -0.5, 0.078125),
    }


def convolve(field, weight):
    result = lax.conv_general_dilated(field.astype(jnp.float32)[None], weight.astype(jnp.float32), (1, 1, 1), [(2, 0), (1, 1), (1, 1)], dimension_numbers=("NDHWC", "DHWIO", "NDHWC"))
    return result[0]


def reference(latent, entry_kernel, middle_kernel, upper_kernel):
    bottom = convolve(latent, entry_kernel).astype(jnp.bfloat16)
    middle = convolve(bottom, middle_kernel)
    section_one = (bottom.astype(jnp.float32) + jax.nn.silu(middle)).astype(jnp.bfloat16)
    enlarged = jnp.repeat(jnp.repeat(section_one, 2, axis=1), 2, axis=2)
    return jax.nn.silu(convolve(enlarged, upper_kernel)).astype(jnp.bfloat16)
```

```python
import jax
import jax.numpy as jnp
from jax import lax
from jax.experimental import pallas as pl
from jax.experimental.pallas import tpu as pltpu
from jax.sharding import PartitionSpec as P

BF = jnp.bfloat16
F32 = jnp.float32
VM = pltpu.VMEM
SUB = 16

PAIRS = ((0, 2, -1), (1, 2, 1), (2, 1, -1), (1, 3, -1))


def swap(block, axis, distance):
    size = lax.axis_size(axis)
    return lax.ppermute(block, axis, [(i, i ^ distance) for i in range(size)])


def swap_across(block, axis):
    size = lax.axis_size(axis)
    pairs = []
    for i in range(size):
        k = (((i // 2) + 1) ^ 1) - 1
        if 0 <= k < size // 2:
            pairs.append((i, 2 * k + i % 2))
    return lax.ppermute(block, axis, pairs)


def silu(v):
    h = 0.5 * v
    return h + h * jnp.tanh(h)


def mm(a, b):
    return jnp.dot(a, b, preferred_element_type=F32)


def filtered(g0, g1, g2):
    s = 0.5 * (g0 + g2)
    h = 0.5 * g1
    return (g0, s + h, s - h, g2)


def summed(g0, g1, g2):
    return (-g0, (g0 + g1) + g2, g2)


def prepare_kernel(entry, mid, up, w_entry, w_mid, w_up):
    cin = entry.shape[0] // 27
    w_entry[...] = jnp.zeros_like(w_entry)
    for k in range(3):
        for a in range(3):
            for b in range(3):
                for c in range(3):
                    row = c * 256 + (a * 5 + b + k) * cin
                    at = (a * 9 + b * 3 + c) * cin
                    w_entry[k, row : row + cin, :] = entry[at : at + cin, :]
    ch = mid.shape[1]

    def step(i, carry):
        rows = pl.ds(pl.multiple_of(i * SUB, SUB), SUB)
        for c in range(3):
            g = [[mid[a * 9 + b * 3 + c, rows, :].astype(F32) for b in range(3)] for a in range(3)]
            t = [filtered(*[g[a][b] for a in range(3)]) for b in range(3)]
            to = pl.ds(pl.multiple_of(c * ch + i * SUB, SUB), SUB)
            for p in range(4):
                for q, value in enumerate(filtered(*[t[b][p] for b in range(3)])):
                    w_mid[p * 4 + q, to, :] = value.astype(BF)
        for a in range(3):
            g = [[up[a * 9 + b * 3 + c, rows, :].astype(F32) for c in range(3)] for b in range(3)]
            t = [summed(*[g[b][c] for b in range(3)]) for c in range(3)]
            to = pl.ds(pl.multiple_of(a * ch + i * SUB, SUB), SUB)
            for p in range(3):
                for q, value in enumerate(summed(*[t[c][p] for c in range(3)])):
                    w_up[p * 3 + q, to, :] = value.astype(BF)
        return carry

    lax.fori_loop(0, ch // SUB, step, 0)


def make_main(n_rows, cin, width, ch, n_x):
    k_tiles = width // SUB
    wide = width + 2 * SUB
    lanes = -(-width // 128) * 128

    def edged(y):
        s = lax.broadcasted_iota(jnp.int32, (SUB, ch), 0)
        before = pltpu.roll(y[width - SUB :], 1, 0)
        after = pltpu.roll(y[:SUB], SUB - 1, 0)
        before = jnp.where(s == 0, 0.0, before)
        after = jnp.where(s == SUB - 1, 0.0, after)
        return jnp.concatenate([before, y, after], axis=0).astype(BF)

    def three(v):
        return jnp.concatenate([v[c * SUB : c * SUB + width] for c in range(3)], axis=1)

    def kernel(where_ref, own, za, zb, w_entry, w_mid, w_up, out, lat, ent, bot, tmid, acc, sec, drow, prod, fin, done, sem):
        tm = where_ref[0]
        rw = where_ref[1]
        lat[...] = jnp.zeros_like(lat)
        z_odd = (rw // 2) % 2 == 1
        r_odd = rw % 2 == 1
        t_odd = tm % 2 == 1
        for bo in range(4):
            other_c = 1 - bo % 2
            if bo == 3:
                dx = 0
            elif bo == 2:
                dx = jnp.where(t_odd, 0, 1)
            elif bo == 1:
                dx = 1
            else:
                dx = jnp.where(t_odd, 1, min(2, n_x - 1))
            t_ok = tm - 3 + bo >= 0
            for ro in range(-2, 3):
                row_ok = jnp.logical_and(rw + ro >= 0, rw + ro < n_rows)
                ok = jnp.logical_and(t_ok, row_ok)
                y = ro % 2
                use_a = z_odd if ro < 0 else jnp.logical_not(z_odd)
                if ro == 0:
                    stays = None
                elif ro == -1:
                    stays = r_odd
                elif ro == 1:
                    stays = jnp.logical_not(r_odd)
                else:
                    stays = False
                for f in range(2):
                    for row in ((1,) if ro == -2 else (0,) if ro == 2 else (0, 1)):
                        h = 2 * (ro + 2) + row - 1
                        at = (y, dx, other_c, f, row)
                        if ro == 0:
                            v = own[at]
                        else:
                            v = jnp.where(use_a, za[at], zb[at])
                            if stays is not False:
                                v = jnp.where(stays, own[at], v)
                        lat[2 * bo + f, h * cin : (h + 1) * cin, :width] = jnp.where(ok, v, jnp.zeros_like(v))
        p = lax.broadcasted_iota(jnp.int32, (wide, lanes), 0)
        j = lax.broadcasted_iota(jnp.int32, (wide, lanes), 1)
        hit = jnp.logical_and(j == (p % SUB) * k_tiles + p // SUB - 1, j < width)
        order = jnp.where(hit, 1.0, 0.0).astype(BF)
        pad = jnp.zeros((ch - 15 * cin, lanes), BF)
        for f in range(6):
            for u in range(2):
                rows = [lat[f + a, 3 * u * cin : (3 * u + 5) * cin, :] for a in range(3)]
                stack = jnp.concatenate(rows + [pad], axis=0)
                patch = lax.dot_general(order, stack, (((1,), (1,)), ((), ())), preferred_element_type=F32)
                ent[f, u] = patch.astype(BF)
        for k in range(3):
            for u in range(2):
                r = 3 * u + k
                left = jnp.concatenate([three(ent[f, u]) for f in range(6)], axis=0)
                y = mm(left, w_entry[k])
                line = 2 * rw - 2 + r
                keep = jnp.where(jnp.logical_and(line >= 0, line < 2 * n_rows), 1.0, 0.0)
                y = y * keep
                for f in range(6):
                    bot[f, r] = edged(y[f * width : (f + 1) * width])
        for t in range(2):
            for k, (i0, i1, sign) in enumerate(PAIRS):
                for r in range(6):
                    v0, v1 = bot[2 * t + i0, r], bot[2 * t + i1, r]
                    tmid[k, t, r] = v0 + v1 if sign > 0 else v0 - v1
        for k in range(4):
            m = [prod.at[k % 2, q] for q in range(4)]
            for q, (i0, i1, sign) in enumerate(PAIRS):
                left = []
                for t in range(2):
                    for u in range(2):
                        v0, v1 = tmid[k, t, 2 * u + i0], tmid[k, t, 2 * u + i1]
                        left.append(three(v0 + v1 if sign > 0 else v0 - v1))
                m[q][...] = mm(jnp.concatenate(left, axis=0), w_mid[k * 4 + q])
            for q in range(2):
                value = (m[0][...] + m[1][...]) + m[2][...] if q == 0 else (m[1][...] - m[2][...]) - m[3][...]
                if k == 0:
                    acc[0, q] = value
                elif k == 1:
                    acc[0, q] = acc[0, q] + value
                    acc[1, q] = value
                elif k == 2:
                    acc[0, q] = acc[0, q] + value
                    acc[1, q] = acc[1, q] - value
                else:
                    acc[1, q] = acc[1, q] - value
        for t in range(2):
            for u in range(2):
                at = (2 * t + u) * width
                for dt in range(2):
                    for dr in range(2):
                        s, v = 2 * t + dt, 2 * u + dr
                        b = bot[s + 2, v + 1, SUB : SUB + width, :].astype(F32)
                        y = b + silu(acc[dt, dr, at : at + width, :])
                        line = 2 * rw - 1 + v
                        keep = jnp.where(jnp.logical_and(line >= 0, line < 2 * n_rows), 1.0, 0.0)
                        sec[s, v] = edged(y * keep)
        for s in range(4):
            for m in range(3):
                drow[s, m] = sec[s, m + 1] - sec[s, m]
        copies = []
        for t in range(2):
            for i in range(2):
                rows = (
                    [drow[t + a, i] for a in range(3)],
                    [sec[t + a, i + 1] for a in range(3)],
                    [drow[t + a, i + 1] for a in range(3)],
                )
                q = []
                for al in range(3):
                    diff = [x[SUB:] - x[:-SUB] for x in rows[al]]
                    mid_x = [x[SUB : SUB + width] for x in rows[al]]
                    m = [prod.at[(t * 2 + i) % 2, al, be * width : (be + 1) * width] for be in range(3)]
                    m[0][...] = mm(jnp.concatenate([d[:width] for d in diff], axis=1), w_up[al * 3])
                    m[1][...] = mm(jnp.concatenate(mid_x, axis=1), w_up[al * 3 + 1])
                    m[2][...] = mm(jnp.concatenate([d[SUB:] for d in diff], axis=1), w_up[al * 3 + 2])
                    q.append(m)
                for pr in range(2):
                    n = (t * 2 + i) * 2 + pr
                    for pc in range(2):
                        y = silu((q[1][1][...] + q[1][2 * pc][...]) + (q[2 * pr][1][...] + q[2 * pr][2 * pc][...]))
                        for kk in range(k_tiles):
                            for half in range(ch // 128):
                                part = slice(half * 128, half * 128 + 128)
                                fin[n % 2, half, pl.ds(2 * kk + pc, SUB, stride=2 * k_tiles), :] = y[kk * SUB : (kk + 1) * SUB, part]
                    even = jnp.concatenate([fin[n % 2, half] for half in range(ch // 128)], axis=1)
                    done[n] = even.astype(BF)
                    copy = pltpu.make_async_copy(done.at[n], out.at[t, 2 * i + pr], sem.at[n])
                    copy.start()
                    copies.append(copy)
        for copy in copies:
            copy.wait()

    return kernel


def per_device(latent, entry_kernel, middle_kernel, upper_kernel):
    n_tm, n_rows = lax.axis_size("tm"), lax.axis_size("rows")
    frames, height, width, cin = latent.shape
    ch = middle_kernel.shape[-1]
    wide = width + 2 * SUB
    vmem = pl.BlockSpec(memory_space=VM)
    w_entry, w_mid, w_up = pl.pallas_call(
        prepare_kernel,
        out_shape=(
            jax.ShapeDtypeStruct((3, 3 * 256, ch), BF),
            jax.ShapeDtypeStruct((16, 3 * ch, ch), BF),
            jax.ShapeDtypeStruct((9, 3 * ch, ch), BF),
        ),
        in_specs=[vmem] * 3,
        out_specs=(vmem,) * 3,
        compiler_params=pltpu.CompilerParams(vmem_limit_bytes=24 * 2**20),
        name="prepare",
    )(
        entry_kernel.reshape(27 * cin, ch),
        middle_kernel.reshape(27, ch, ch),
        upper_kernel.reshape(27, ch, ch),
    )
    x = jnp.transpose(latent, (0, 1, 3, 2))
    x = jnp.stack([x, swap(x, "tm", 1)])
    steps = [d for d in (2, 4) if d < n_tm]
    x = jnp.stack([x] + [lax.ppermute(x, "tm", [(i, (i + d) % n_tm) for i in range(n_tm)]) for d in steps])
    x = jnp.stack([x, swap(x, "rows", 1)])
    za, zb = swap(x, "rows", 2), swap_across(x, "rows")
    where = jnp.stack([lax.axis_index("tm"), lax.axis_index("rows")]).astype(jnp.int32)
    kernel = make_main(n_rows, cin, width, ch, 1 + len(steps))
    return pl.pallas_call(
        kernel,
        out_shape=jax.ShapeDtypeStruct((frames, 2 * height, 2 * width, ch), BF),
        in_specs=[pl.BlockSpec(memory_space=pltpu.SMEM)] + [vmem] * 6,
        out_specs=pl.BlockSpec(memory_space=pl.ANY),
        scratch_shapes=[
            VM((8, 8 * cin, -(-width // 128) * 128), BF),
            VM((6, 2, wide, ch), BF),
            VM((6, 6, wide, ch), BF),
            VM((4, 2, 6, wide, ch), BF),
            VM((2, 2, 4 * width, ch), F32),
            VM((4, 4, wide, ch), BF),
            VM((4, 3, wide, ch), BF),
            VM((2, 4, 4 * width, ch), F32),
            VM((2, ch // 128, 2 * width, 128), F32),
            VM((8, 2 * width, ch), BF),
            pltpu.SemaphoreType.DMA((8,)),
        ],
        compiler_params=pltpu.CompilerParams(vmem_limit_bytes=36 * 2**20),
        name="section",
    )(where, x, za, zb, w_entry, w_mid, w_up)


def solution(mesh):
    return jax.shard_map(
        per_device,
        mesh=mesh,
        in_specs=(P("tm", "rows", None, None), P(), P(), P()),
        out_specs=P("tm", "rows", None, None),
        check_vma=False,
    )
```

```python
import jax
import jax.numpy as jnp
from jax import lax
from jax.experimental import pallas as pl
from jax.experimental.pallas import tpu as pltpu
from jax.sharding import PartitionSpec as P

BF = jnp.bfloat16
F32 = jnp.float32
VM = pltpu.VMEM
SUB = 16

PAIRS = ((0, 2, -1), (1, 2, 1), (2, 1, -1), (1, 3, -1))


def swap(block, axis, distance):
    size = lax.axis_size(axis)
    return lax.ppermute(block, axis, [(i, i ^ distance) for i in range(size)])


def swap_across(block, axis):
    size = lax.axis_size(axis)
    pairs = []
    for i in range(size):
        k = (((i // 2) + 1) ^ 1) - 1
        if 0 <= k < size // 2:
            pairs.append((i, 2 * k + i % 2))
    return lax.ppermute(block, axis, pairs)


def silu(v):
    h = 0.5 * v
    return h + h * jnp.tanh(h)


def mm(a, b):
    return jnp.dot(a, b, preferred_element_type=F32)


def filtered(g0, g1, g2):
    s = 0.5 * (g0 + g2)
    h = 0.5 * g1
    return (g0, s + h, s - h, g2)


def summed(g0, g1, g2):
    return (-g0, (g0 + g1) + g2, g2)


CHUNKS = 4


def fetch(raw, here, sems):
    size = raw.shape[1] // CHUNKS
    copies = []
    for n in range(CHUNKS):
        part = pl.ds(n * size, size)
        copy = pltpu.make_async_copy(raw.at[:, part], here.at[:, part], sems.at[n])
        copy.start()
        copies.append(copy)
    return copies


def prepare_middle(entry, raw, w_entry, w_mid, mid, sems):
    ch = raw.shape[1]
    steps = ch // SUB // CHUNKS
    copies = fetch(raw, mid, sems)
    cin = entry.shape[0] // 27
    w_entry[...] = jnp.zeros_like(w_entry)
    for k in range(3):
        for a in range(3):
            for b in range(3):
                for c in range(3):
                    row = c * ch + (a * 5 + b + k) * cin
                    at = (a * 9 + b * 3 + c) * cin
                    w_entry[k, row : row + cin, :] = entry[at : at + cin, :]
    for n, copy in enumerate(copies):
        copy.wait()

        def step(i, carry):
            at = pl.multiple_of((n * steps + i) * SUB, SUB)
            for c in range(3):
                g = [[mid[a * 9 + b * 3 + c, pl.ds(at, SUB), :].astype(F32) for b in range(3)] for a in range(3)]
                t = [filtered(*[g[a][b] for a in range(3)]) for b in range(3)]
                for p in range(4):
                    for q, value in enumerate(filtered(*[t[b][p] for b in range(3)])):
                        w_mid[p * 4 + q, pl.ds(c * ch + at, SUB), :] = value.astype(BF)
            return carry

        lax.fori_loop(0, steps, step, 0)


def prepare_upper(raw, w_up, up, sems):
    ch = raw.shape[1]
    steps = ch // SUB // CHUNKS
    for n, copy in enumerate(fetch(raw, up, sems)):
        copy.wait()

        def step(i, carry):
            at = pl.multiple_of((n * steps + i) * SUB, SUB)
            for a in range(3):
                g = [[up[a * 9 + b * 3 + c, pl.ds(at, SUB), :].astype(F32) for c in range(3)] for b in range(3)]
                t = [summed(*[g[b][c] for b in range(3)]) for c in range(3)]
                for p in range(3):
                    for q, value in enumerate(summed(*[t[c][p] for c in range(3)])):
                        w_up[p * 3 + q, pl.ds(a * ch + at, SUB), :] = value.astype(BF)
            return carry

        lax.fori_loop(0, steps, step, 0)


def pack(latent, packed):
    blocks, _, _ = latent.shape
    packed[:blocks] = latent[:, :, :128]
    packed[blocks] = jnp.concatenate([latent[i, :, 128:] for i in range(blocks)], axis=1)


def make_main(n_rows, cin, width, ch, n_x):
    k_tiles = width // SUB
    wide = width + 2 * SUB
    lanes = -(-width // 128) * 128

    def edged(y):
        s = lax.broadcasted_iota(jnp.int32, (SUB, ch), 0)
        before = pltpu.roll(y[width - SUB :], 1, 0)
        after = pltpu.roll(y[:SUB], SUB - 1, 0)
        before = jnp.where(s == 0, 0.0, before)
        after = jnp.where(s == SUB - 1, 0.0, after)
        return jnp.concatenate([before, y, after], axis=0).astype(BF)

    def three(v):
        return jnp.concatenate([v[c * SUB : c * SUB + width] for c in range(3)], axis=1)

    def kernel(where_ref, own, za, zb, w_entry, w_mid, w_up, out, lat, ent, bot, tmid, acc, sec, drow, prod, fin, done, sem):
        tm = where_ref[0]
        rw = where_ref[1]
        lat[...] = jnp.zeros_like(lat)
        z_odd = (rw // 2) % 2 == 1
        r_odd = rw % 2 == 1
        t_odd = tm % 2 == 1
        for bo in range(4):
            other_c = 1 - bo % 2
            if bo == 3:
                dx = 0
            elif bo == 2:
                dx = jnp.where(t_odd, 0, 1)
            elif bo == 1:
                dx = 1
            else:
                dx = jnp.where(t_odd, 1, min(2, n_x - 1))
            t_ok = tm - 3 + bo >= 0
            for ro in range(-2, 3):
                row_ok = jnp.logical_and(rw + ro >= 0, rw + ro < n_rows)
                ok = jnp.logical_and(t_ok, row_ok)
                y = ro % 2
                use_a = z_odd if ro < 0 else jnp.logical_not(z_odd)
                if ro == 0:
                    stays = None
                elif ro == -1:
                    stays = r_odd
                elif ro == 1:
                    stays = jnp.logical_not(r_odd)
                else:
                    stays = False
                for f in range(2):
                    for row in ((1,) if ro == -2 else (0,) if ro == 2 else (0, 1)):
                        h = 2 * (ro + 2) + row - 1
                        n = 2 * f + row
                        for tile in (n, 4):
                            at = (y, dx, other_c, tile)
                            if ro == 0:
                                v = own[at]
                            else:
                                v = jnp.where(use_a, za[at], zb[at])
                                if stays is not False:
                                    v = jnp.where(stays, own[at], v)
                            v = jnp.where(ok, v, jnp.zeros_like(v))
                            if tile == n:
                                lat[2 * bo + f, h * cin : (h + 1) * cin, :128] = v
                            else:
                                v = v[:, n * (width - 128) : (n + 1) * (width - 128)]
                                lat[2 * bo + f, h * cin : (h + 1) * cin, 128:width] = v
        p = lax.broadcasted_iota(jnp.int32, (wide, lanes), 0)
        j = lax.broadcasted_iota(jnp.int32, (wide, lanes), 1)
        hit = jnp.logical_and(j == (p % SUB) * k_tiles + p // SUB - 1, j < width)
        order = jnp.where(hit, 1.0, 0.0).astype(BF)
        pad = jnp.zeros((ch - 15 * cin, lanes), BF)
        for f in range(6):
            for u in range(2):
                rows = [lat[f + a, 3 * u * cin : (3 * u + 5) * cin, :] for a in range(3)]
                stack = jnp.concatenate(rows + [pad], axis=0)
                patch = lax.dot_general(order, stack, (((1,), (1,)), ((), ())), preferred_element_type=F32)
                ent[f, u] = patch.astype(BF)
        for k in range(3):
            for u in range(2):
                r = 3 * u + k
                left = jnp.concatenate([three(ent[f, u]) for f in range(6)], axis=0)
                y = mm(left, w_entry[k])
                line = 2 * rw - 2 + r
                keep = jnp.where(jnp.logical_and(line >= 0, line < 2 * n_rows), 1.0, 0.0)
                y = y * keep
                for f in range(6):
                    bot[f, r] = edged(y[f * width : (f + 1) * width])
        for t in range(2):
            for k, (i0, i1, sign) in enumerate(PAIRS):
                for r in range(6):
                    v0, v1 = bot[2 * t + i0, r], bot[2 * t + i1, r]
                    tmid[k, t, r] = v0 + v1 if sign > 0 else v0 - v1
            for k in range(4):
                m = [prod.at[k % 2, q, t] for q in range(4)]
                for q, (i0, i1, sign) in enumerate(PAIRS):
                    left = []
                    for u in range(2):
                        v0, v1 = tmid[k, t, 2 * u + i0], tmid[k, t, 2 * u + i1]
                        left.append(three(v0 + v1 if sign > 0 else v0 - v1))
                    m[q][...] = mm(jnp.concatenate(left, axis=0), w_mid[k * 4 + q])
                for q in range(2):
                    value = (m[0][...] + m[1][...]) + m[2][...] if q == 0 else (m[1][...] - m[2][...]) - m[3][...]
                    if k == 0:
                        acc[t, 0, q] = value
                    elif k == 1:
                        acc[t, 0, q] = acc[t, 0, q] + value
                        acc[t, 1, q] = value
                    elif k == 2:
                        acc[t, 0, q] = acc[t, 0, q] + value
                        acc[t, 1, q] = acc[t, 1, q] - value
                    else:
                        acc[t, 1, q] = acc[t, 1, q] - value
            for u in range(2):
                for dt in range(2):
                    for dr in range(2):
                        s, v = 2 * t + dt, 2 * u + dr
                        b = bot[s + 2, v + 1, SUB : SUB + width, :].astype(F32)
                        y = b + silu(acc[t, dt, dr, u * width : (u + 1) * width, :])
                        line = 2 * rw - 1 + v
                        keep = jnp.where(jnp.logical_and(line >= 0, line < 2 * n_rows), 1.0, 0.0)
                        sec[s, v] = edged(y * keep)
        for s in range(4):
            for m in range(3):
                drow[s, m] = sec[s, m + 1] - sec[s, m]
        copies = []
        for t in range(2):
            for i in range(2):
                rows = (
                    [drow[t + a, i] for a in range(3)],
                    [sec[t + a, i + 1] for a in range(3)],
                    [drow[t + a, i + 1] for a in range(3)],
                )
                q = []
                for al in range(3):
                    diff = [x[SUB:] - x[:-SUB] for x in rows[al]]
                    mid_x = [x[SUB : SUB + width] for x in rows[al]]
                    m = [prod.at[i, al, be // 2, be % 2 * width : (be % 2 + 1) * width] for be in range(3)]
                    m[0][...] = mm(jnp.concatenate([d[:width] for d in diff], axis=1), w_up[al * 3])
                    m[1][...] = mm(jnp.concatenate(mid_x, axis=1), w_up[al * 3 + 1])
                    m[2][...] = mm(jnp.concatenate([d[SUB:] for d in diff], axis=1), w_up[al * 3 + 2])
                    q.append(m)
                for pr in range(2):
                    n = (t * 2 + i) * 2 + pr
                    for pc in range(2):
                        y = silu((q[1][1][...] + q[1][2 * pc][...]) + (q[2 * pr][1][...] + q[2 * pr][2 * pc][...]))
                        for kk in range(k_tiles):
                            for half in range(ch // 128):
                                part = slice(half * 128, half * 128 + 128)
                                fin[n % 2, half, pl.ds(2 * kk + pc, SUB, stride=2 * k_tiles), :] = y[kk * SUB : (kk + 1) * SUB, part]
                    even = jnp.concatenate([fin[n % 2, half] for half in range(ch // 128)], axis=1)
                    done[n] = even.astype(BF)
                    copy = pltpu.make_async_copy(done.at[n], out.at[t, 2 * i + pr], sem.at[n])
                    copy.start()
                    copies.append(copy)
        for copy in copies:
            copy.wait()

    return kernel


def per_device(latent, entry_kernel, middle_kernel, upper_kernel):
    n_tm, n_rows = lax.axis_size("tm"), lax.axis_size("rows")
    frames, height, width, cin = latent.shape
    ch = middle_kernel.shape[-1]
    wide = width + 2 * SUB
    vmem = pl.BlockSpec(memory_space=VM)
    small = pltpu.CompilerParams(vmem_limit_bytes=6 * 2**20)
    keep = lambda w: pltpu.with_memory_space_constraint(w, pltpu.HBM)
    hbm = pl.BlockSpec(memory_space=pltpu.HBM)
    fetched = [VM((27, ch, ch), BF), pltpu.SemaphoreType.DMA((CHUNKS,))]
    w_entry, w_mid = pl.pallas_call(
        prepare_middle,
        out_shape=(VM((3, 3 * ch, ch), BF), VM((16, 3 * ch, ch), BF)),
        in_specs=[vmem, hbm],
        out_specs=(vmem, vmem),
        scratch_shapes=fetched,
        compiler_params=small,
        name="prepare_middle",
    )(entry_kernel.reshape(27 * cin, ch), keep(middle_kernel.reshape(27, ch, ch)))
    w_up = pl.pallas_call(
        prepare_upper,
        out_shape=VM((9, 3 * ch, ch), BF),
        in_specs=[hbm],
        out_specs=vmem,
        scratch_shapes=fetched,
        compiler_params=small,
        name="prepare_upper",
    )(keep(upper_kernel.reshape(27, ch, ch)))
    x = jnp.transpose(latent, (0, 1, 3, 2)).reshape(frames * height, cin, width)
    x = pl.pallas_call(
        pack,
        out_shape=jax.ShapeDtypeStruct((frames * height + 1, cin, 128), BF),
        in_specs=[vmem],
        out_specs=vmem,
        compiler_params=small,
        name="pack",
    )(x)
    other = swap(x, "tm", 1)
    x = jnp.stack([x, other])
    steps = [d for d in (2, 4) if d < n_tm]
    others = [lax.ppermute(x, "tm", [(i, (i + d) % n_tm) for i in range(n_tm)]) for d in steps]
    x = jnp.stack([x] + others)
    other = swap(x, "rows", 1)
    x = jnp.stack([x, other])
    za = swap(x, "rows", 2)
    zb = swap_across(x, "rows")
    where = jnp.stack([lax.axis_index("tm"), lax.axis_index("rows")]).astype(jnp.int32)
    kernel = make_main(n_rows, cin, width, ch, 1 + len(steps))
    return pl.pallas_call(
        kernel,
        out_shape=jax.ShapeDtypeStruct((frames, 2 * height, 2 * width, ch), BF),
        in_specs=[pl.BlockSpec(memory_space=pltpu.SMEM)] + [vmem] * 6,
        out_specs=pl.BlockSpec(memory_space=pl.ANY),
        scratch_shapes=[
            VM((8, 8 * cin, -(-width // 128) * 128), BF),
            VM((6, 2, wide, ch), BF),
            VM((6, 6, wide, ch), BF),
            VM((4, 2, 6, wide, ch), BF),
            VM((2, 2, 2, 2 * width, ch), F32),
            VM((4, 4, wide, ch), BF),
            VM((4, 3, wide, ch), BF),
            VM((2, 4, 2, 2 * width, ch), F32),
            VM((2, ch // 128, 2 * width, 128), F32),
            VM((8, 2 * width, ch), BF),
            pltpu.SemaphoreType.DMA((8,)),
        ],
        compiler_params=pltpu.CompilerParams(vmem_limit_bytes=32 * 2**20),
        name="section",
    )(where, x, za, zb, w_entry, w_mid, w_up)


def solution(mesh):
    return jax.shard_map(
        per_device,
        mesh=mesh,
        in_specs=(P("tm", "rows", None, None), P(), P(), P()),
        out_specs=P("tm", "rows", None, None),
        check_vma=False,
    )
```

```python
import jax
import jax.numpy as jnp
from jax import lax
from jax.experimental import pallas as pl
from jax.experimental.pallas import tpu as pltpu
from jax.sharding import PartitionSpec as P

BF = jnp.bfloat16
F32 = jnp.float32
VM = pltpu.VMEM
SUB = 16

PAIRS = ((0, 2, -1), (1, 2, 1), (2, 1, -1), (1, 3, -1))


def swap(block, axis, distance):
    size = lax.axis_size(axis)
    return lax.ppermute(block, axis, [(i, i ^ distance) for i in range(size)])


def swap_across(block, axis):
    size = lax.axis_size(axis)
    pairs = []
    for i in range(size):
        k = (((i // 2) + 1) ^ 1) - 1
        if 0 <= k < size // 2:
            pairs.append((i, 2 * k + i % 2))
    return lax.ppermute(block, axis, pairs)


def silu(v):
    h = 0.5 * v
    return h + h * jnp.tanh(h)


def mm(a, b):
    return jnp.dot(a, b, preferred_element_type=F32)


def filtered(g0, g1, g2):
    s = 0.5 * (g0 + g2)
    h = 0.5 * g1
    return (g0, s + h, s - h, g2)


def summed(g0, g1, g2):
    return (-g0, (g0 + g1) + g2, g2)


CHUNKS = 4


def fetch(raw, here, sems):
    size = raw.shape[1] // CHUNKS
    copies = []
    for n in range(CHUNKS):
        part = pl.ds(n * size, size)
        copy = pltpu.make_async_copy(raw.at[:, part], here.at[:, part], sems.at[n])
        copy.start()
        copies.append(copy)
    return copies


def prepare_middle(first, raw, w_entry, w_mid, mid, sems, entry, sem):
    taken = pltpu.make_async_copy(first, entry, sem)
    taken.start()
    ch = raw.shape[1]
    steps = ch // SUB // CHUNKS
    copies = fetch(raw, mid, sems)
    cin = entry.shape[0] // 27
    w_entry[...] = jnp.zeros_like(w_entry)
    taken.wait()
    for k in range(3):
        for a in range(3):
            for b in range(3):
                for c in range(3):
                    row = c * ch + (a * 5 + b + k) * cin
                    at = (a * 9 + b * 3 + c) * cin
                    w_entry[k, row : row + cin, :] = entry[at : at + cin, :]
    for n, copy in enumerate(copies):
        copy.wait()

        def step(i, carry):
            at = pl.multiple_of((n * steps + i) * SUB, SUB)
            for c in range(3):
                g = [[mid[a * 9 + b * 3 + c, pl.ds(at, SUB), :].astype(F32) for b in range(3)] for a in range(3)]
                t = [filtered(*[g[a][b] for a in range(3)]) for b in range(3)]
                for p in range(4):
                    for q, value in enumerate(filtered(*[t[b][p] for b in range(3)])):
                        w_mid[p * 4 + q, pl.ds(c * ch + at, SUB), :] = value.astype(BF)
            return carry

        lax.fori_loop(0, steps, step, 0)


def prepare_upper(raw, w_up, up, sems):
    ch = raw.shape[1]
    steps = ch // SUB // CHUNKS
    for n, copy in enumerate(fetch(raw, up, sems)):
        copy.wait()

        def step(i, carry):
            at = pl.multiple_of((n * steps + i) * SUB, SUB)
            for a in range(3):
                g = [[up[a * 9 + b * 3 + c, pl.ds(at, SUB), :].astype(F32) for c in range(3)] for b in range(3)]
                t = [summed(*[g[b][c] for b in range(3)]) for c in range(3)]
                for p in range(3):
                    for q, value in enumerate(summed(*[t[c][p] for c in range(3)])):
                        w_up[p * 3 + q, pl.ds(a * ch + at, SUB), :] = value.astype(BF)
            return carry

        lax.fori_loop(0, steps, step, 0)


def pack(latent, packed):
    blocks, _, _ = latent.shape
    packed[:blocks] = latent[:, :, :128]
    packed[blocks] = jnp.concatenate([latent[i, :, 128:] for i in range(blocks)], axis=1)


def make_main(n_rows, cin, width, ch, n_x):
    k_tiles = width // SUB
    wide = width + 2 * SUB
    lanes = -(-width // 128) * 128

    def edged(y):
        s = lax.broadcasted_iota(jnp.int32, (SUB, ch), 0)
        before = pltpu.roll(y[width - SUB :], 1, 0)
        after = pltpu.roll(y[:SUB], SUB - 1, 0)
        before = jnp.where(s == 0, 0.0, before)
        after = jnp.where(s == SUB - 1, 0.0, after)
        return jnp.concatenate([before, y, after], axis=0).astype(BF)

    def three(v):
        return jnp.concatenate([v[c * SUB : c * SUB + width] for c in range(3)], axis=1)

    def kernel(where_ref, own0, own1, za0, za1, zb0, zb1, w_entry, w_mid, w_up, out, lat, ent, bot, tmid, acc, sec, drow, prod, fin, done, sem):
        tm = where_ref[0]
        rw = where_ref[1]
        lat[...] = jnp.zeros_like(lat)
        z_odd = (rw // 2) % 2 == 1
        r_odd = rw % 2 == 1
        t_odd = tm % 2 == 1
        for bo in range(4):
            own, za, zb = (own0, za0, zb0) if bo % 2 else (own1, za1, zb1)
            if bo == 3:
                dx = 0
            elif bo == 2:
                dx = jnp.where(t_odd, 0, 1)
            elif bo == 1:
                dx = 1
            else:
                dx = jnp.where(t_odd, 1, min(2, n_x - 1))
            t_ok = tm - 3 + bo >= 0
            for ro in range(-2, 3):
                row_ok = jnp.logical_and(rw + ro >= 0, rw + ro < n_rows)
                ok = jnp.logical_and(t_ok, row_ok)
                y = ro % 2
                use_a = z_odd if ro < 0 else jnp.logical_not(z_odd)
                if ro == 0:
                    stays = None
                elif ro == -1:
                    stays = r_odd
                elif ro == 1:
                    stays = jnp.logical_not(r_odd)
                else:
                    stays = False
                for f in range(2):
                    for row in ((1,) if ro == -2 else (0,) if ro == 2 else (0, 1)):
                        h = 2 * (ro + 2) + row - 1
                        n = 2 * f + row
                        for tile in (n, 4):
                            at = (y, dx, tile)
                            if ro == 0:
                                v = own[at]
                            else:
                                v = jnp.where(use_a, za[at], zb[at])
                                if stays is not False:
                                    v = jnp.where(stays, own[at], v)
                            v = jnp.where(ok, v, jnp.zeros_like(v))
                            if tile == n:
                                lat[2 * bo + f, h * cin : (h + 1) * cin, :128] = v
                            else:
                                v = v[:, n * (width - 128) : (n + 1) * (width - 128)]
                                lat[2 * bo + f, h * cin : (h + 1) * cin, 128:width] = v
        p = lax.broadcasted_iota(jnp.int32, (wide, lanes), 0)
        j = lax.broadcasted_iota(jnp.int32, (wide, lanes), 1)
        hit = jnp.logical_and(j == (p % SUB) * k_tiles + p // SUB - 1, j < width)
        order = jnp.where(hit, 1.0, 0.0).astype(BF)
        pad = jnp.zeros((ch - 15 * cin, lanes), BF)
        for f in range(6):
            for u in range(2):
                rows = [lat[f + a, 3 * u * cin : (3 * u + 5) * cin, :] for a in range(3)]
                stack = jnp.concatenate(rows + [pad], axis=0)
                patch = lax.dot_general(order, stack, (((1,), (1,)), ((), ())), preferred_element_type=F32)
                ent[f, u] = patch.astype(BF)
        for k in range(3):
            for u in range(2):
                r = 3 * u + k
                left = jnp.concatenate([three(ent[f, u]) for f in range(6)], axis=0)
                y = mm(left, w_entry[k])
                line = 2 * rw - 2 + r
                keep = jnp.where(jnp.logical_and(line >= 0, line < 2 * n_rows), 1.0, 0.0)
                y = y * keep
                for f in range(6):
                    bot[f, r] = edged(y[f * width : (f + 1) * width])
        for t in range(2):
            for k, (i0, i1, sign) in enumerate(PAIRS):
                for r in range(6):
                    v0, v1 = bot[2 * t + i0, r], bot[2 * t + i1, r]
                    tmid[k, t, r] = v0 + v1 if sign > 0 else v0 - v1
            for k in range(4):
                m = [prod.at[k % 2, q, t] for q in range(4)]
                for q, (i0, i1, sign) in enumerate(PAIRS):
                    left = []
                    for u in range(2):
                        v0, v1 = tmid[k, t, 2 * u + i0], tmid[k, t, 2 * u + i1]
                        left.append(three(v0 + v1 if sign > 0 else v0 - v1))
                    m[q][...] = mm(jnp.concatenate(left, axis=0), w_mid[k * 4 + q])
                for q in range(2):
                    value = (m[0][...] + m[1][...]) + m[2][...] if q == 0 else (m[1][...] - m[2][...]) - m[3][...]
                    if k == 0:
                        acc[t, 0, q] = value
                    elif k == 1:
                        acc[t, 0, q] = acc[t, 0, q] + value
                        acc[t, 1, q] = value
                    elif k == 2:
                        acc[t, 0, q] = acc[t, 0, q] + value
                        acc[t, 1, q] = acc[t, 1, q] - value
                    else:
                        acc[t, 1, q] = acc[t, 1, q] - value
            for u in range(2):
                for dt in range(2):
                    for dr in range(2):
                        s, v = 2 * t + dt, 2 * u + dr
                        b = bot[s + 2, v + 1, SUB : SUB + width, :].astype(F32)
                        y = b + silu(acc[t, dt, dr, u * width : (u + 1) * width, :])
                        line = 2 * rw - 1 + v
                        keep = jnp.where(jnp.logical_and(line >= 0, line < 2 * n_rows), 1.0, 0.0)
                        sec[s, v] = edged(y * keep)
        for s in range(4):
            for m in range(3):
                drow[s, m] = sec[s, m + 1] - sec[s, m]
        copies = []
        for t in range(2):
            for i in range(2):
                rows = (
                    [drow[t + a, i] for a in range(3)],
                    [sec[t + a, i + 1] for a in range(3)],
                    [drow[t + a, i + 1] for a in range(3)],
                )
                q = []
                for al in range(3):
                    diff = [x[SUB:] - x[:-SUB] for x in rows[al]]
                    mid_x = [x[SUB : SUB + width] for x in rows[al]]
                    m = [prod.at[i, al, be // 2, be % 2 * width : (be % 2 + 1) * width] for be in range(3)]
                    m[0][...] = mm(jnp.concatenate([d[:width] for d in diff], axis=1), w_up[al * 3])
                    m[1][...] = mm(jnp.concatenate(mid_x, axis=1), w_up[al * 3 + 1])
                    m[2][...] = mm(jnp.concatenate([d[SUB:] for d in diff], axis=1), w_up[al * 3 + 2])
                    q.append(m)
                for pr in range(2):
                    n = (t * 2 + i) * 2 + pr
                    for pc in range(2):
                        y = silu((q[1][1][...] + q[1][2 * pc][...]) + (q[2 * pr][1][...] + q[2 * pr][2 * pc][...]))
                        for kk in range(k_tiles):
                            for half in range(ch // 128):
                                part = slice(half * 128, half * 128 + 128)
                                fin[n % 2, half, pl.ds(2 * kk + pc, SUB, stride=2 * k_tiles), :] = y[kk * SUB : (kk + 1) * SUB, part]
                    even = jnp.concatenate([fin[n % 2, half] for half in range(ch // 128)], axis=1)
                    done[n] = even.astype(BF)
                    copy = pltpu.make_async_copy(done.at[n], out.at[t, 2 * i + pr], sem.at[n])
                    copy.start()
                    copies.append(copy)
        for copy in copies:
            copy.wait()

    return kernel


def per_device(latent, entry_kernel, middle_kernel, upper_kernel):
    n_tm, n_rows = lax.axis_size("tm"), lax.axis_size("rows")
    frames, height, width, cin = latent.shape
    ch = middle_kernel.shape[-1]
    wide = width + 2 * SUB
    vmem = pl.BlockSpec(memory_space=VM)
    small = pltpu.CompilerParams(vmem_limit_bytes=6 * 2**20)
    keep = lambda w: pltpu.with_memory_space_constraint(w, pltpu.HBM)
    hbm = pl.BlockSpec(memory_space=pltpu.HBM)
    fetched = [VM((27, ch, ch), BF), pltpu.SemaphoreType.DMA((CHUNKS,))]
    w_entry, w_mid = pl.pallas_call(
        prepare_middle,
        out_shape=(VM((3, 3 * ch, ch), BF), VM((16, 3 * ch, ch), BF)),
        in_specs=[hbm, hbm],
        out_specs=(vmem, vmem),
        scratch_shapes=fetched + [VM((27 * cin, ch), BF), pltpu.SemaphoreType.DMA(())],
        compiler_params=small,
        name="prepare_middle",
    )(keep(entry_kernel.reshape(27 * cin, ch)), keep(middle_kernel.reshape(27, ch, ch)))
    w_up = pl.pallas_call(
        prepare_upper,
        out_shape=VM((9, 3 * ch, ch), BF),
        in_specs=[hbm],
        out_specs=vmem,
        scratch_shapes=fetched,
        compiler_params=small,
        name="prepare_upper",
    )(keep(upper_kernel.reshape(27, ch, ch)))
    x = jnp.transpose(latent, (0, 1, 3, 2)).reshape(frames * height, cin, width)
    x = pl.pallas_call(
        pack,
        out_shape=jax.ShapeDtypeStruct((frames * height + 1, cin, 128), BF),
        in_specs=[vmem],
        out_specs=vmem,
        compiler_params=small,
        name="pack",
    )(x)
    steps = [d for d in (2, 4) if d < n_tm]
    others = [lax.ppermute(x, "tm", [(i, (i + d) % n_tm) for i in range(n_tm)]) for d in steps]
    x = jnp.stack([x] + others)
    other = swap(x, "rows", 1)
    x = jnp.stack([x, other])
    za = swap(x, "rows", 2)
    zb = swap_across(x, "rows")
    both = [(v, swap(v, "tm", 1)) for v in (x, za, zb)]
    where = jnp.stack([lax.axis_index("tm"), lax.axis_index("rows")]).astype(jnp.int32)
    kernel = make_main(n_rows, cin, width, ch, 1 + len(steps))
    return pl.pallas_call(
        kernel,
        out_shape=jax.ShapeDtypeStruct((frames, 2 * height, 2 * width, ch), BF),
        in_specs=[pl.BlockSpec(memory_space=pltpu.SMEM)] + [vmem] * 9,
        out_specs=pl.BlockSpec(memory_space=pl.ANY),
        scratch_shapes=[
            VM((8, 8 * cin, -(-width // 128) * 128), BF),
            VM((6, 2, wide, ch), BF),
            VM((6, 6, wide, ch), BF),
            VM((4, 2, 6, wide, ch), BF),
            VM((2, 2, 2, 2 * width, ch), F32),
            VM((4, 4, wide, ch), BF),
            VM((4, 3, wide, ch), BF),
            VM((2, 4, 2, 2 * width, ch), F32),
            VM((2, ch // 128, 2 * width, 128), F32),
            VM((8, 2 * width, ch), BF),
            pltpu.SemaphoreType.DMA((8,)),
        ],
        compiler_params=pltpu.CompilerParams(vmem_limit_bytes=26 * 2**20),
        name="section",
    )(where, *both[0], *both[1], *both[2], w_entry, w_mid, w_up)


def solution(mesh):
    return jax.shard_map(
        per_device,
        mesh=mesh,
        in_specs=(P("tm", "rows", None, None), P(), P(), P()),
        out_specs=P("tm", "rows", None, None),
        check_vma=False,
    )
```

```python
import jax
import jax.numpy as jnp
from jax import lax
from jax.experimental import pallas as pl
from jax.experimental.pallas import tpu as pltpu
from jax.sharding import PartitionSpec as P

BF = jnp.bfloat16
F32 = jnp.float32
VM = pltpu.VMEM
SUB = 16

PAIRS = ((0, 2, -1), (1, 2, 1), (2, 1, -1), (1, 3, -1))


def swap(block, axis, distance):
    size = lax.axis_size(axis)
    return lax.ppermute(block, axis, [(i, i ^ distance) for i in range(size)])


def swap_across(block, axis):
    size = lax.axis_size(axis)
    pairs = []
    for i in range(size):
        k = (((i // 2) + 1) ^ 1) - 1
        if 0 <= k < size // 2:
            pairs.append((i, 2 * k + i % 2))
    return lax.ppermute(block, axis, pairs)


def silu(v):
    h = 0.5 * v
    return h + h * jnp.tanh(h)


def mm(a, b):
    return jnp.dot(a, b, preferred_element_type=F32)


def filtered(g0, g1, g2):
    s = g0 + g2
    return (g0, s + g1, s - g1, g2)


def summed(g0, g1, g2):
    return (-g0, (g0 + g1) + g2, g2)


CHUNKS = 4
SUMS = ((0, 1), (1, 0), (1, 1), (1, 2), (2, 1))
CORNERS = ((0, 0), (0, 2), (2, 0), (2, 2))


def fetch(raw, here, sems):
    size = raw.shape[1] // CHUNKS
    copies = []
    for n in range(CHUNKS):
        part = pl.ds(n * size, size)
        copy = pltpu.make_async_copy(raw.at[:, part], here.at[:, part], sems.at[n])
        copy.start()
        copies.append(copy)
    return copies


def prepare_middle(first, raw, w_entry, w_mid, mid, sems, entry, sem):
    taken = pltpu.make_async_copy(first, entry, sem)
    taken.start()
    ch = raw.shape[1]
    steps = ch // SUB // CHUNKS
    copies = fetch(raw, mid, sems)
    cin = entry.shape[0] // 27
    w_entry[...] = jnp.zeros_like(w_entry)
    taken.wait()
    for k in range(3):
        for a in range(3):
            for b in range(3):
                for c in range(3):
                    row = c * ch + (a * 5 + b + k) * cin
                    at = (a * 9 + b * 3 + c) * cin
                    w_entry[k, row : row + cin, :] = entry[at : at + cin, :]
    for n, copy in enumerate(copies):
        copy.wait()

        def step(i, carry):
            at = pl.multiple_of((n * steps + i) * SUB, SUB)
            for c in range(3):
                g = [[mid[a * 9 + b * 3 + c, pl.ds(at, SUB), :].astype(F32) for b in range(3)] for a in range(3)]
                t = [filtered(*[g[a][b] for a in range(3)]) for b in range(3)]
                for p in range(4):
                    for q, value in enumerate(filtered(*[t[b][p] for b in range(3)])):
                        scale = 0.5 * (0.5 if p in (1, 2) else 1.0) * (0.5 if q in (1, 2) else 1.0)
                        w_mid[p * 4 + q, pl.ds(c * ch + at, SUB), :] = value.astype(BF) * jnp.asarray(scale, BF)
            return carry

        lax.fori_loop(0, steps, step, 0)


def prepare_upper(raw, w_up, up, sems):
    ch = raw.shape[1]
    steps = ch // SUB // CHUNKS
    for n, copy in enumerate(fetch(raw, up, sems)):
        copy.wait()

        def step(i, carry):
            at = pl.multiple_of((n * steps + i) * SUB, SUB)
            for a in range(3):
                g = [[up[a * 9 + b * 3 + c, pl.ds(at, SUB), :].astype(F32) for c in range(3)] for b in range(3)]
                t = [summed(*[g[b][c] for b in range(3)]) for c in range(3)]
                s = [summed(*[t[c][p] for c in range(3)]) for p in range(3)]
                for n_out, (p, q) in enumerate(SUMS):
                    w_up[n_out, pl.ds(a * ch + at, SUB), :] = s[p][q].astype(BF)
            return carry

        lax.fori_loop(0, steps, step, 0)


def bring(latent, here):
    here[...] = latent[...]


def pack(*refs):
    packed = refs[-1]
    for n, latent in enumerate(refs[:-1]):
        blocks = latent.shape[0]
        packed[n, :blocks] = latent[:, :, :128]
        packed[n, blocks] = jnp.concatenate([latent[i, :, 128:] for i in range(blocks)], axis=1)


def make_main(n_rows, cin, width, ch, n_x):
    k_tiles = width // SUB
    wide = width + 2 * SUB
    lanes = -(-width // 128) * 128

    def edged(y):
        s = lax.broadcasted_iota(jnp.int32, (SUB, ch), 0)
        before = pltpu.roll(y[width - SUB :], 1, 0)
        after = pltpu.roll(y[:SUB], SUB - 1, 0)
        before = jnp.where(s == 0, 0.0, before)
        after = jnp.where(s == SUB - 1, 0.0, after)
        return jnp.concatenate([before, y, after], axis=0).astype(BF)

    def three(v):
        return jnp.concatenate([v[c * SUB : c * SUB + width] for c in range(3)], axis=1)

    def kernel(where_ref, own0, own1, za0, za1, zb0, zb1, w_entry, w_mid, w_up, raw, out, lat, ent, bot, tmid, acc, sec, drow, prod, fin, done, corner, sem, raw_sem):
        fetched = []
        for n, (b, c) in enumerate(CORNERS):
            for a in range(3):
                to = corner.at[n, a * ch : (a + 1) * ch]
                fetched.append(pltpu.make_async_copy(raw.at[a * 9 + b * 3 + c], to, raw_sem.at[3 * n + a]))
        for copy in fetched:
            copy.start()
        tm = where_ref[0]
        rw = where_ref[1]
        lat[...] = jnp.zeros_like(lat)
        z_odd = (rw // 2) % 2 == 1
        r_odd = rw % 2 == 1
        t_odd = tm % 2 == 1
        for bo in range(4):
            own, za, zb = (own0, za0, zb0) if bo % 2 else (own1, za1, zb1)
            if bo == 3:
                dx = 0
            elif bo == 2:
                dx = jnp.where(t_odd, 0, 1)
            elif bo == 1:
                dx = 1
            else:
                dx = jnp.where(t_odd, 1, min(2, n_x - 1))
            t_ok = tm - 3 + bo >= 0
            for ro in range(-2, 3):
                row_ok = jnp.logical_and(rw + ro >= 0, rw + ro < n_rows)
                ok = jnp.logical_and(t_ok, row_ok)
                y = ro % 2
                use_a = z_odd if ro < 0 else jnp.logical_not(z_odd)
                if ro == 0:
                    stays = None
                elif ro == -1:
                    stays = r_odd
                elif ro == 1:
                    stays = jnp.logical_not(r_odd)
                else:
                    stays = False
                for f in range(2):
                    for row in ((1,) if ro == -2 else (0,) if ro == 2 else (0, 1)):
                        h = 2 * (ro + 2) + row - 1
                        n = 2 * f + row
                        for tile in (n, 4):
                            at = (y, dx, tile)
                            if ro == 0:
                                v = own[at]
                            else:
                                v = jnp.where(use_a, za[at], zb[at])
                                if stays is not False:
                                    v = jnp.where(stays, own[at], v)
                            v = jnp.where(ok, v, jnp.zeros_like(v))
                            if tile == n:
                                lat[2 * bo + f, h * cin : (h + 1) * cin, :128] = v
                            else:
                                v = v[:, n * (width - 128) : (n + 1) * (width - 128)]
                                lat[2 * bo + f, h * cin : (h + 1) * cin, 128:width] = v
        p = lax.broadcasted_iota(jnp.int32, (wide, lanes), 0)
        j = lax.broadcasted_iota(jnp.int32, (wide, lanes), 1)
        hit = jnp.logical_and(j == (p % SUB) * k_tiles + p // SUB - 1, j < width)
        order = jnp.where(hit, 1.0, 0.0).astype(BF)
        pad = jnp.zeros((ch - 15 * cin, lanes), BF)
        for f in range(6):
            for u in range(2):
                rows = [lat[f + a, 3 * u * cin : (3 * u + 5) * cin, :] for a in range(3)]
                stack = jnp.concatenate(rows + [pad], axis=0)
                patch = lax.dot_general(order, stack, (((1,), (1,)), ((), ())), preferred_element_type=F32)
                ent[f, u] = patch.astype(BF)
        for k in range(3):
            for u in range(2):
                r = 3 * u + k
                left = jnp.concatenate([three(ent[f, u]) for f in range(6)], axis=0)
                y = mm(left, w_entry[k])
                if r not in (2, 3):
                    line = 2 * rw - 2 + r
                    y = y * jnp.where(jnp.logical_and(line >= 0, line < 2 * n_rows), 1.0, 0.0)
                for f in range(6):
                    bot[f, r] = edged(y[f * width : (f + 1) * width])
        for t in range(2):
            for k, (i0, i1, sign) in enumerate(PAIRS):
                for r in range(6):
                    v0, v1 = bot[2 * t + i0, r], bot[2 * t + i1, r]
                    tmid[k, t, r] = v0 + v1 if sign > 0 else v0 - v1
            for k in range(4):
                m = [prod.at[k % 2, q, t] for q in range(4)]
                for q, (i0, i1, sign) in enumerate(PAIRS):
                    left = []
                    for u in range(2):
                        v0, v1 = tmid[k, t, 2 * u + i0], tmid[k, t, 2 * u + i1]
                        left.append(three(v0 + v1 if sign > 0 else v0 - v1))
                    m[q][...] = mm(jnp.concatenate(left, axis=0), w_mid[k * 4 + q])
                for q in range(2):
                    value = (m[0][...] + m[1][...]) + m[2][...] if q == 0 else (m[1][...] - m[2][...]) - m[3][...]
                    if k == 0:
                        acc[t, 0, q] = value
                    elif k == 1:
                        acc[t, 0, q] = acc[t, 0, q] + value
                        acc[t, 1, q] = value
                    elif k == 2:
                        acc[t, 0, q] = acc[t, 0, q] + value
                        acc[t, 1, q] = acc[t, 1, q] - value
                    else:
                        acc[t, 1, q] = acc[t, 1, q] - value
            for u in range(2):
                for dt in range(2):
                    for dr in range(2):
                        s, v = 2 * t + dt, 2 * u + dr
                        b = bot[s + 2, v + 1, SUB : SUB + width, :].astype(F32)
                        half = acc[t, dt, dr, u * width : (u + 1) * width, :]
                        y = b + half + half * jnp.tanh(half)
                        if v in (0, 3):
                            line = 2 * rw - 1 + v
                            y = y * jnp.where(jnp.logical_and(line >= 0, line < 2 * n_rows), 1.0, 0.0)
                        sec[s, v] = edged(y)

        def weight(al, be):
            return corner[CORNERS.index((al, be))] if (al, be) in CORNERS else w_up[SUMS.index((al, be))]

        for s in range(4):
            for m in range(3):
                drow[s, m] = sec[s, m + 1] - sec[s, m]
        for copy in fetched:
            copy.wait()
        copies = []
        for t in range(2):
            for i in range(2):
                rows = (
                    [drow[t + a, i] for a in range(3)],
                    [sec[t + a, i + 1] for a in range(3)],
                    [drow[t + a, i + 1] for a in range(3)],
                )
                q = []
                for al in range(3):
                    diff = [x[SUB:] - x[:-SUB] for x in rows[al]]
                    mid_x = [x[SUB : SUB + width] for x in rows[al]]
                    m = [prod.at[i, al, be // 2, be % 2 * width : (be % 2 + 1) * width] for be in range(3)]
                    m[0][...] = mm(jnp.concatenate([d[:width] for d in diff], axis=1), weight(al, 0))
                    m[1][...] = mm(jnp.concatenate(mid_x, axis=1), weight(al, 1))
                    m[2][...] = mm(jnp.concatenate([d[SUB:] for d in diff], axis=1), weight(al, 2))
                    q.append(m)
                for pr in range(2):
                    n = (t * 2 + i) * 2 + pr
                    for pc in range(2):
                        y = (q[1][1][...] + q[1][2 * pc][...]) + q[2 * pr][1][...]
                        last = q[2 * pr][2 * pc][...]
                        y = silu(y + last if pr == pc else y - last)
                        for kk in range(k_tiles):
                            for half in range(ch // 128):
                                part = slice(half * 128, half * 128 + 128)
                                fin[n % 2, half, pl.ds(2 * kk + pc, SUB, stride=2 * k_tiles), :] = y[kk * SUB : (kk + 1) * SUB, part]
                    even = jnp.concatenate([fin[n % 2, half, : 2 * width] for half in range(ch // 128)], axis=1)
                    done[n] = even.astype(BF)
                    copy = pltpu.make_async_copy(done.at[n], out.at[t, 2 * i + pr], sem.at[n])
                    copy.start()
                    copies.append(copy)
        for copy in copies:
            copy.wait()

    return kernel


def per_device(latent, entry_kernel, middle_kernel, upper_kernel):
    n_tm, n_rows = lax.axis_size("tm"), lax.axis_size("rows")
    frames, height, width, cin = latent.shape
    ch = middle_kernel.shape[-1]
    wide = width + 2 * SUB
    vmem = pl.BlockSpec(memory_space=VM)
    small = pltpu.CompilerParams(vmem_limit_bytes=6 * 2**20)
    keep = lambda w: pltpu.with_memory_space_constraint(w, pltpu.HBM)
    hbm = pl.BlockSpec(memory_space=pltpu.HBM)
    fetched = [VM((27, ch, ch), BF), pltpu.SemaphoreType.DMA((CHUNKS,))]
    w_entry, w_mid = pl.pallas_call(
        prepare_middle,
        out_shape=(VM((3, 3 * ch, ch), BF), VM((16, 3 * ch, ch), BF)),
        in_specs=[hbm, hbm],
        out_specs=(vmem, vmem),
        scratch_shapes=fetched + [VM((27 * cin, ch), BF), pltpu.SemaphoreType.DMA(())],
        compiler_params=small,
        name="prepare_middle",
    )(keep(entry_kernel.reshape(27 * cin, ch)), keep(middle_kernel.reshape(27, ch, ch)))
    w_up = pl.pallas_call(
        prepare_upper,
        out_shape=VM((5, 3 * ch, ch), BF),
        in_specs=[hbm],
        out_specs=vmem,
        scratch_shapes=fetched,
        compiler_params=small,
        name="prepare_upper",
    )(keep(upper_kernel.reshape(27, ch, ch)))
    x = jnp.transpose(latent, (0, 1, 3, 2)).reshape(frames * height, cin, width)
    steps = [d for d in (2, 4) if d < n_tm]
    others = [lax.ppermute(x, "tm", [(i, (i + d) % n_tm) for i in range(n_tm)]) for d in steps]
    x = pl.pallas_call(
        bring,
        out_shape=VM((frames * height, cin, width), BF),
        in_specs=[vmem],
        out_specs=vmem,
        compiler_params=small,
        name="bring",
    )(keep(x))
    x = pl.pallas_call(
        pack,
        out_shape=jax.ShapeDtypeStruct((1 + len(steps), frames * height + 1, cin, 128), BF),
        in_specs=[vmem] * (1 + len(steps)),
        out_specs=vmem,
        compiler_params=small,
        name="pack",
    )(x, *others)
    other = swap(x, "rows", 1)
    x = jnp.stack([x, other])
    za = swap(x, "rows", 2)
    zb = swap_across(x, "rows")
    both = [(x, swap(x, "tm", 1))]
    both += [(v, swap(v, "tm", 1)) for v in (za, zb)]
    where = jnp.stack([lax.axis_index("tm"), lax.axis_index("rows")]).astype(jnp.int32)
    kernel = make_main(n_rows, cin, width, ch, 1 + len(steps))
    return pl.pallas_call(
        kernel,
        out_shape=jax.ShapeDtypeStruct((frames, 2 * height, 2 * width, ch), BF),
        in_specs=[pl.BlockSpec(memory_space=pltpu.SMEM)] + [vmem] * 9 + [hbm],
        out_specs=pl.BlockSpec(memory_space=pl.ANY),
        scratch_shapes=[
            VM((8, 8 * cin, -(-width // 128) * 128), BF),
            VM((6, 2, wide, ch), BF),
            VM((6, 6, wide, ch), BF),
            VM((4, 2, 6, wide, ch), BF),
            VM((2, 2, 2, 2 * width, ch), F32),
            VM((4, 4, wide, ch), BF),
            VM((4, 3, wide, ch), BF),
            VM((2, 4, 2, 2 * width, ch), F32),
            VM((2, ch // 128, 2 * width + 2 * (width // SUB), 128), F32),
            VM((8, 2 * width, ch), BF),
            VM((4, 3 * ch, ch), BF),
            pltpu.SemaphoreType.DMA((8,)),
            pltpu.SemaphoreType.DMA((12,)),
        ],
        compiler_params=pltpu.CompilerParams(vmem_limit_bytes=28 * 2**20),
        name="section",
    )(where, *both[0], *both[1], *both[2], w_entry, w_mid, w_up, keep(upper_kernel.reshape(27, ch, ch)))


def solution(mesh):
    return jax.shard_map(
        per_device,
        mesh=mesh,
        in_specs=(P("tm", "rows", None, None), P(), P(), P()),
        out_specs=P("tm", "rows", None, None),
        check_vma=False,
    )
```
